128 devices in a mesh: sens: 8 (over x, y_hi), par: 16 (over y_lo, z, core).
Axes of the slice: x: 4, y: 4 (y_hi: 2, y_lo: 2; y = y_hi * 2 + y_lo), z: 4, core: 2. Of those that a mesh axis runs over, the one named last changes fastest.
Arguments:
- records: float32 [16, 600, 224], P(None, 'sens'), may hold values from -6 to 6
- spec_real: float32 [225, 600, 2048], P(None, 'sens', 'par'), may hold values from -0.109375 to 0.109375
- spec_imag: float32 [225, 600, 2048], P(None, 'sens', 'par'), may hold values from -0.109375 to 0.109375
- prior_cov: float32 [224, 224], replicated, as said below
- sensor_map: int32 [600], replicated, may hold values from 0 to 599, each once
- inverse_rows: float32 [768, 224, 600], P('sens', 'par'), may hold values from -0.015625 to 0.015625
Outputs:
- update: float32 [16, 768], P('par', 'sens')
The draws below stay inside these ranges and needn't reach their ends.
Inputs may be any that keep to these rules, and one draw needn't show every extreme that they name: prior_cov is symmetric. sensor_map names every sensor once.
All inputs are finite; a program needn't handle non-finite values.
Results may differ from the reference program's by a relative error of at most 0.00013.
Values sent between devices are 32-bit elements; how exact they have to be, the bound alone decides.
A program may use at most 128 MiB of HBM per device.

```python
import math
import jax
import jax.numpy as jnp
from jax import lax

SENS = 600
NT = 224
COLS = 16
NF = 225
PAR = 2048
ROWS = 768


def draw_prior_cov(key, part):
    sample = jax.random.normal(key, (NT, NT), jnp.float32)
    symmetric = (sample + sample.T) * (0.5 / math.sqrt(NT))
    return symmetric + 2.0 * jnp.eye(NT, dtype=jnp.float32)


def levels(key, extent, cuts, smallest, high):
    loudness, own = 1.0, jax.random.fold_in(key, 6)
    for position, shards_of in cuts:
        heights = jnp.exp(jax.random.uniform(jax.random.fold_in(own, position), (shards_of,), jnp.float32, smallest / len(cuts), high / len(cuts)))
        loudness = loudness * jnp.repeat(heights, extent[position] // shards_of).reshape([-1 if axis == position else 1 for axis in range(len(extent))])
    return loudness


def bell_draw(rng, shape, scale, most, shards=(), kind=jnp.bfloat16):
    drawn = scale * jax.random.normal(rng, shape, jnp.float32)
    if shards:
        drawn = drawn * levels(rng, shape, shards, -0.22, 0.18)
    return jnp.clip(drawn, -most, most).astype(kind)


def setup_inputs(seed: int = 0) -> dict:
    streams_of = jax.random.split(jax.random.key(seed), 7)
    records = bell_draw(streams_of[0], (COLS, SENS, NT), 1.0, 6.0, ((1, 8),), jnp.float32)
    spec_real = bell_draw(streams_of[1], (NF, SENS, PAR), (2 * SENS + PAR) ** -0.5, 0.109375, ((1, 8), (2, 16)), jnp.float32)
    spec_imag = bell_draw(streams_of[2], (NF, SENS, PAR), (2 * SENS + PAR) ** -0.5, 0.109375, ((1, 8), (2, 16)), jnp.float32)
    prior_cov = draw_prior_cov(jax.random.fold_in(streams_of[6], 71), 0)
    sensor_map = jax.random.permutation(streams_of[4], SENS).astype(jnp.int32)
    inverse_rows = bell_draw(streams_of[5], (ROWS, NT, SENS), (NT * SENS) ** -0.5, 0.015625, ((0, 8), (1, 16)), jnp.float32)
    return dict(records=records, spec_real=spec_real, spec_imag=spec_imag, prior_cov=prior_cov, sensor_map=sensor_map, inverse_rows=inverse_rows)


highest = lax.Precision.HIGHEST


def reference(records, spec_real, spec_imag, prior_cov, sensor_map, inverse_rows):
    length = 2 * NT
    rec_spec = jnp.fft.rfft(records, n=length, axis=2)
    rec_real = jnp.real(rec_spec)
    rec_imag = jnp.imag(rec_spec)
    adj_real = jnp.einsum('csw,wsp->cpw', rec_real, spec_real, precision=highest) + jnp.einsum('csw,wsp->cpw', rec_imag, spec_imag, precision=highest)
    adj_imag = jnp.einsum('csw,wsp->cpw', rec_imag, spec_real, precision=highest) - jnp.einsum('csw,wsp->cpw', rec_real, spec_imag, precision=highest)
    adjoint = jnp.fft.irfft(lax.complex(adj_real, adj_imag), n=length, axis=2)[:, :, :NT]
    prior_field = jnp.dot(adjoint, prior_cov, precision=highest, preferred_element_type=jnp.float32)
    field_spec = jnp.fft.rfft(prior_field, n=length, axis=2)
    field_real = jnp.real(field_spec)
    field_imag = jnp.imag(field_spec)
    pred_real = jnp.einsum('cpw,wsp->csw', field_real, spec_real, precision=highest) - jnp.einsum('cpw,wsp->csw', field_imag, spec_imag, precision=highest)
    pred_imag = jnp.einsum('cpw,wsp->csw', field_imag, spec_real, precision=highest) + jnp.einsum('cpw,wsp->csw', field_real, spec_imag, precision=highest)
    predicted = jnp.fft.irfft(lax.complex(pred_real, pred_imag), n=length, axis=2)[:, :, :NT]
    permuted = jnp.take(predicted, sensor_map, axis=1)
    return jnp.einsum('rtk,ckt->cr', inverse_rows, permuted, precision=highest)
```

```python
import functools
import math

import jax
import jax.numpy as jnp
import ml_dtypes
import numpy as np
from jax import lax
from jax.experimental import pallas as pl
from jax.experimental.pallas import tpu as pltpu
from jax.sharding import PartitionSpec as P

MESH = pl.DeviceIdType.MESH
F32, BF16 = jnp.float32, jnp.bfloat16
VMEM = pl.BlockSpec(memory_space=pltpu.VMEM)
ANY = pl.BlockSpec(memory_space=pl.ANY)

COLS, NT, NF = 16, 224, 225
SD, PD = 75, 128
SPAD = 80
FR = 232
ROWS2 = 2 * COLS
CHUNK = 25
NCHUNK = NF // CHUNK
UNROLL = 5


def split_np(table):
    high = table.astype(np.float32).astype(ml_dtypes.bfloat16)
    low = (table - high.astype(np.float64)).astype(np.float32).astype(ml_dtypes.bfloat16)
    return high, low


def tables():
    length = 2 * NT
    w = np.arange(NF)
    t = np.arange(NT)
    phase = (np.outer(w, t) % length) * (2.0 * math.pi / length)
    fwd = np.zeros((2 * FR, NT))
    fwd[:NF] = np.cos(phase)
    fwd[FR : FR + NF] = -np.sin(phase)
    weight = np.where((w == 0) | (w == NT), 1.0, 2.0) / length
    inv = np.zeros((NT, 512))
    inv[:, :NF] = np.cos(phase).T * weight
    inv[:, 256 : 256 + NF] = -np.sin(phase).T * weight
    return (*split_np(fwd), *split_np(inv))


def split(x):
    high = x.astype(BF16)
    return high, (x - high.astype(F32)).astype(BF16)


def dot(a, b, dims=((1,), (0,))):
    return lax.dot_general(a, b, (dims, ((), ())), preferred_element_type=F32)


NT_DIMS = ((1,), (1,))
LIMIT = 60 * 2**20


def dot3(a, b, dims=((1,), (0,))):
    return dot(a[0], b[0], dims) + (dot(a[1], b[0], dims) + dot(a[0], b[1], dims))


def params(**more):
    return pltpu.CompilerParams(vmem_limit_bytes=LIMIT, **more)


def start_specs(sr_hbm, si_hbm, sr, si, sems):
    @pl.loop(0, SD)
    def _(s):
        pltpu.make_async_copy(sr_hbm.at[s], sr.at[:, s, :], sems.at[0]).start()
        pltpu.make_async_copy(si_hbm.at[s], si.at[:, s, :], sems.at[1]).start()


def wait_specs(sr_hbm, si_hbm, sr, si, sems):
    blank = jnp.zeros((CHUNK, SPAD - SD, PD), F32)

    @pl.loop(0, NCHUNK)
    def _(i):
        sr[pl.ds(i * CHUNK, CHUNK), SD:SPAD, :] = blank
        si[pl.ds(i * CHUNK, CHUNK), SD:SPAD, :] = blank

    @pl.loop(0, SD)
    def _(s):
        pltpu.make_async_copy(sr_hbm.at[s], sr.at[:, s, :], sems.at[0]).wait()
        pltpu.make_async_copy(si_hbm.at[s], si.at[:, s, :], sems.at[1]).wait()


def over_frequencies(step):
    @pl.loop(0, NF // UNROLL)
    def _(j):
        for u in range(UNROLL):
            step(j * UNROLL + u)


def part_rows(c):
    return (c, COLS + c)


def to_samples(yn, idh, idl, q):
    total = None
    for part in range(2):
        both = split(jnp.concatenate([yn[part * COLS + 2 * q], yn[part * COLS + 2 * q + 1]], axis=1))
        table = (idh[:, part * 256 : (part + 1) * 256], idl[:, part * 256 : (part + 1) * 256])
        term = dot3(table, both)
        total = term if total is None else total + term
    return total


def put_spectrum(xn, x, res, q, sem):
    for half in range(2):
        for part, row in enumerate(part_rows(2 * q + half)):
            xn[row, 0:FR, :] = res[part * FR : (part + 1) * FR, half * 128 : (half + 1) * 128]
            pltpu.make_async_copy(xn.at[row, pl.ds(0, NF)], x.at[:, row, :], sem).start()


def wait_rows(xn, x, sem):
    @pl.loop(0, ROWS2)
    def _(row):
        pltpu.make_async_copy(xn.at[row, pl.ds(0, NF)], x.at[:, row, :], sem).wait()


def start_columns(y, yn, sems):
    @pl.loop(0, COLS // 2)
    def _(q):
        for half in range(2):
            for row in part_rows(2 * q + half):
                pltpu.make_async_copy(y.at[:, row, :], yn.at[row, pl.ds(0, NF)], sems.at[q]).start()


def wait_columns(y, yn, sems, q):
    for half in range(2):
        for row in part_rows(2 * q + half):
            pltpu.make_async_copy(y.at[:, row, :], yn.at[row, pl.ds(0, NF)], sems.at[q]).wait()


def clear_tails(yn):
    @pl.loop(0, ROWS2)
    def _(row):
        yn[row, NF:256, :] = jnp.zeros((256 - NF, 128), F32)


def adjoint_kernel(
    rec_in, sr_hbm, si_hbm, fdh, fdl, idh, idl, out, sr, si, x, y, xn, flat, rec, sems, rsem, xsem, ysem
):
    start_specs(sr_hbm, si_hbm, sr, si, sems)
    flat[0] = rec_in[:, :, 0:128]
    flat[1, :, :, 0 : NT - 128] = rec_in[:, :, 128:NT]

    def row_copy(side, c):
        return pltpu.make_async_copy(
            flat.at[side, :, c, :], rec.at[side, c, pl.ds(0, SD)], rsem.at[side]
        )

    @pl.loop(0, COLS)
    def _(c):
        row_copy(0, c).start()
        row_copy(1, c).start()
        rec[0, c, SD:128, :] = jnp.zeros((128 - SD, 128), F32)
        rec[1, c, SD:128, :] = jnp.zeros((128 - SD, 128), F32)

    @pl.loop(0, COLS)
    def _(c):
        row_copy(0, c).wait()
        row_copy(1, c).wait()

    @pl.loop(0, COLS // 2)
    def _(q):
        sides = [rec[side, pl.ds(2 * q, 2)].reshape(256, 128) for side in range(2)]
        both = split(jnp.concatenate([sides[0], sides[1][:, : NT - 128]], axis=1))
        put_spectrum(xn, x, dot3((fdh[...], fdl[...]), both, NT_DIMS), q, xsem)

    wait_rows(xn, x, xsem)
    wait_specs(sr_hbm, si_hbm, sr, si, sems)
    clear_tails(xn)

    def step(w):
        ah, al = split(x[w][:, :SPAD])
        both = split(jnp.concatenate([sr[w], si[w]], axis=1))
        wide = dot(jnp.concatenate([ah, al], axis=0), both[0])
        p = wide[:ROWS2] + (wide[ROWS2:] + dot(ah, both[1]))
        y[w] = jnp.concatenate(
            [p[:COLS, :PD] + p[COLS:, PD:], p[COLS:, :PD] - p[:COLS, PD:]], axis=0
        )

    over_frequencies(step)
    start_columns(y, xn, ysem)

    @pl.loop(0, COLS // 2)
    def _(q):
        wait_columns(y, xn, ysem, q)
        res = to_samples(xn, idh, idl, q)
        out[2 * q] = res[:, :PD]
        out[2 * q + 1] = res[:, PD:]


def forward_kernel(
    adj, prior, sr_hbm, si_hbm, fdh, fdl, idh, idl, out, sr, si, x, y, xn, on, ph, pl_, sems, xsem, ysem, osem
):
    start_specs(sr_hbm, si_hbm, sr, si, sems)
    high, low = split(dot3((fdh[...], fdl[...]), split(prior[...])))
    ph[...] = high
    pl_[...] = low

    @pl.loop(0, COLS // 2)
    def _(q):
        both = split(jnp.concatenate([adj[2 * q], adj[2 * q + 1]], axis=1))
        put_spectrum(xn, x, dot3((ph[...], pl_[...]), both), q, xsem)

    wait_rows(xn, x, xsem)
    wait_specs(sr_hbm, si_hbm, sr, si, sems)
    clear_tails(xn)

    def step(w):
        fh, fl = split(x[w])
        left = jnp.concatenate(
            [jnp.concatenate([fh, fh], axis=1), jnp.concatenate([fl, jnp.zeros_like(fl)], axis=1)],
            axis=0,
        )
        prods = []
        for s in (sr, si):
            wide = dot(left, jnp.concatenate(split(s[w]), axis=1), NT_DIMS)
            prods.append(wide[:ROWS2] + wide[ROWS2:])
        p, r = prods
        both = jnp.concatenate([p[:COLS] - r[COLS:], p[COLS:] + r[:COLS]], axis=0)
        y[w] = jnp.concatenate([both, jnp.zeros((ROWS2, 128 - SPAD), F32)], axis=1)

    over_frequencies(step)
    start_columns(y, xn, ysem)

    @pl.loop(0, COLS // 2)
    def _(q):
        wait_columns(y, xn, ysem, q)
        res = to_samples(xn, idh, idl, q)
        for half in range(2):
            on[2 * q + half] = res[:, half * 128 : (half + 1) * 128]
            pltpu.make_async_copy(on.at[2 * q + half], out.at[:, 2 * q + half, :], osem).start()

    @pl.loop(0, COLS)
    def _(c):
        pltpu.make_async_copy(on.at[c], out.at[:, c, :], osem).wait()


def spec_scratch():
    return [
        pltpu.VMEM((NF, SPAD, PD), F32),
        pltpu.VMEM((NF, SPAD, PD), F32),
        pltpu.VMEM((NF, ROWS2, 128), F32),
        pltpu.VMEM((NF, ROWS2, 128), F32),
        pltpu.VMEM((ROWS2, 256, 128), F32),
    ]


def adjoint_call(rec, sr, si, tabs):
    return pl.pallas_call(
        adjoint_kernel,
        out_shape=jax.ShapeDtypeStruct((COLS, NT, PD), F32),
        in_specs=[VMEM, ANY, ANY] + [VMEM] * 4,
        out_specs=VMEM,
        scratch_shapes=spec_scratch()
        + [
            pltpu.VMEM((2, SD, COLS, 128), F32),
            pltpu.VMEM((2, COLS, 128, 128), F32),
            pltpu.SemaphoreType.DMA((2,)),
            pltpu.SemaphoreType.DMA((2,)),
            pltpu.SemaphoreType.DMA,
            pltpu.SemaphoreType.DMA((COLS // 2,)),
        ],
        compiler_params=params(),
        name="adjoint",
    )(rec, sr, si, *tabs)


def forward_call(adj, prior, sr, si, tabs):
    return pl.pallas_call(
        forward_kernel,
        out_shape=jax.ShapeDtypeStruct((NT, COLS, 128), F32),
        in_specs=[VMEM, VMEM, ANY, ANY] + [VMEM] * 4,
        out_specs=VMEM,
        scratch_shapes=spec_scratch()
        + [pltpu.VMEM((COLS, NT, 128), F32)]
        + [pltpu.VMEM((2 * FR, NT), BF16)] * 2
        + [
            pltpu.SemaphoreType.DMA((2,)),
            pltpu.SemaphoreType.DMA,
            pltpu.SemaphoreType.DMA((COLS // 2,)),
            pltpu.SemaphoreType.DMA,
        ],
        compiler_params=params(),
        name="forward",
    )(adj, prior, sr, si, *tabs)


def update_kernel(place, gath, inv_hbm, out, inv, perm, sem):
    copy = pltpu.make_async_copy(inv_hbm, inv, sem)
    copy.start()
    steps, rows, keys = inv.shape
    where = place[...]

    @pl.loop(0, gath.shape[0] // 2)
    def _(i):
        row = lax.broadcasted_iota(jnp.int32, (256, keys), 0) + i * 256
        pick = (row == where).astype(F32).astype(BF16)
        high, low = split(jnp.concatenate([gath[2 * i], gath[2 * i + 1]], axis=1))
        term = dot(high, pick) + dot(low, pick)

        @pl.when(i == 0)
        def _():
            perm[...] = term

        @pl.when(i > 0)
        def _():
            perm[...] += term

    copy.wait()
    out[...] = jnp.zeros_like(out)

    @pl.loop(0, steps)
    def _(t):
        at = pl.ds(pl.multiple_of(t * COLS, COLS), COLS)
        out[:, 0:rows] += dot3(split(perm[at, :]), split(inv[t]), NT_DIMS)


def update_call(place, gath, inv):
    return pl.pallas_call(
        update_kernel,
        out_shape=jax.ShapeDtypeStruct((COLS, 128), F32),
        in_specs=[VMEM, VMEM, ANY],
        out_specs=VMEM,
        scratch_shapes=[
            pltpu.VMEM(inv.shape, F32),
            pltpu.VMEM((gath.shape[1], inv.shape[2]), F32),
            pltpu.SemaphoreType.DMA,
        ],
        compiler_params=params(),
        name="update",
    )(place, gath, inv)


def here():
    sens, par = lax.axis_index("sens"), lax.axis_index("par")
    return sens // 2, sens % 2, par // 8, par // 2 % 4, par % 2


def device(x, y_hi, y_lo, z, core):
    return (x * 2 + y_hi, y_lo * 8 + z * 2 + core)


def greet(devices):
    barrier = pltpu.get_barrier_semaphore()
    for d in devices:
        pl.semaphore_signal(barrier, inc=1, device_id=d, device_id_type=MESH)
    pl.semaphore_wait(barrier, len(devices))


class Sender:
    def __init__(self, send_sems, recv_sems):
        self.send_sems, self.recv_sems, self.sent = send_sems, recv_sems, []

    def __call__(self, src, dst, to):
        k = len(self.sent)
        copy = pltpu.make_async_remote_copy(
            src_ref=src,
            dst_ref=dst,
            send_sem=self.send_sems.at[k],
            recv_sem=self.recv_sems.at[k],
            device_id=to,
            device_id_type=MESH,
        )
        copy.start()
        self.sent.append(copy)
        return copy

    def finish(self):
        for copy in self.sent:
            copy.wait_send()


def rows_at(start, size):
    return pl.ds(pl.multiple_of(start, 8), size)


class RingSum:
    def __init__(self, send, data, at, place, up, down, relay, arrive):
        self.send, self.data, self.at, self.place = send, data, at, place
        self.up, self.down, self.relay, self.arrive = up, down, relay, arrive
        nxt, prv, far = (place + 1) % 4, (place + 3) % 4, (place + 2) % 4
        self.nxt, self.prv = nxt, prv
        self.far_up = send(data.at[at(far, 0)], relay.at[0], up)
        self.far_down = send(data.at[at(far, 1)], relay.at[1], down)
        self.near_up = send(data.at[at(nxt, 1)], arrive.at[0], up)
        self.near_down = send(data.at[at(prv, 0)], arrive.at[1], down)

    def pass_on(self):
        self.far_up.wait_recv()
        self.relay[0] = self.relay[0] + self.data[self.at(self.nxt, 0)]
        self.last_up = self.send(self.relay.at[0], self.arrive.at[2], self.up)
        self.far_down.wait_recv()
        self.relay[1] = self.relay[1] + self.data[self.at(self.prv, 1)]
        self.last_down = self.send(self.relay.at[1], self.arrive.at[3], self.down)

    def half(self, h):
        (self.near_down, self.near_up)[h].wait_recv()
        (self.last_up, self.last_down)[h].wait_recv()
        own = self.data[self.at(self.place, h)]
        return own + self.arrive[(1, 0)[h]] + self.arrive[(2, 3)[h]]


class RingSpread:
    def __init__(self, send, data, at, place, up, down):
        self.send, self.data, self.at, self.place, self.up, self.down = send, data, at, place, up, down
        mine = [data.at[at(place, h)] for h in range(2)]
        self.first_up = send(mine[0], mine[0], up)
        self.first_down = send(mine[1], mine[1], down)
        self.second_up = send(mine[1], mine[1], up)
        self.second_down = send(mine[0], mine[0], down)

    def pass_on(self):
        self.first_up.wait_recv()
        piece = self.data.at[self.at((self.place + 3) % 4, 0)]
        self.far_up = self.send(piece, piece, self.up)
        self.first_down.wait_recv()
        piece = self.data.at[self.at((self.place + 1) % 4, 1)]
        self.far_down = self.send(piece, piece, self.down)

    def finish(self):
        for copy in (self.second_up, self.second_down, self.far_up, self.far_down):
            copy.wait_recv()


def sum_all_kernel(a, out, relay_a, arrive_a, swap_a, relay_b, arrive_b, swap_b, half_b, done_a, ssem, rsem):
    x, y_hi, y_lo, z, core = here()
    up = device((x + 1) % 4, y_hi, y_lo, z, core)
    down = device((x + 3) % 4, y_hi, y_lo, z, core)
    over = device(x, 1 - y_hi, y_lo, z, core)
    greet([up, down, over])
    send = Sender(ssem, rsem)
    half_a = relay_a.shape[1]
    quarter_b = relay_b.shape[1]
    start_b = 8 * half_a
    size_b = 8 * quarter_b

    def at_a(q, h):
        return rows_at((2 * q + h) * half_a, half_a)

    def at_half_b(q, h):
        return rows_at((2 * q + h) * quarter_b, quarter_b)

    def at_b(y):
        def at(q, h):
            return rows_at(start_b + y * size_b + (2 * q + h) * quarter_b, quarter_b)

        return at

    theirs = rows_at(start_b + (1 - y_hi) * size_b, size_b)
    ours = rows_at(start_b + y_hi * size_b, size_b)
    to_over_b = send(a.at[theirs], swap_b, over)
    ring_a = RingSum(send, a, at_a, x, up, down, relay_a, arrive_a)
    ring_a.pass_on()
    to_over_b.wait_recv()
    half_b[...] = a[ours] + swap_b[...]
    ring_b = RingSum(send, half_b, at_half_b, x, up, down, relay_b, arrive_b)
    for h in range(2):
        done_a[h] = ring_a.half(h)
    to_over_a = send(done_a.at[1 - y_hi], swap_a, over)
    ring_b.pass_on()
    to_over_a.wait_recv()
    mine = at_a(x, y_hi)
    out[mine] = done_a[y_hi] + swap_a[...]
    back_a = send(out.at[mine], out.at[mine], over)
    place_b = at_b(y_hi)
    for h in range(2):
        out[place_b(x, h)] = ring_b.half(h)
    spread_b = RingSpread(send, out, place_b, x, up, down)
    back_a.wait_recv()
    spread_a = RingSpread(send, out, at_a, x, up, down)
    spread_b.pass_on()
    spread_b.finish()
    back_b = send(out.at[ours], out.at[ours], over)
    spread_a.pass_on()
    spread_a.finish()
    back_b.wait_recv()
    send.finish()


def sum_all_call(a):
    rows = a.shape[0]
    half_a = 272
    quarter_b = (rows - 8 * half_a) // 16
    return pl.pallas_call(
        sum_all_kernel,
        out_shape=jax.ShapeDtypeStruct(a.shape, F32),
        in_specs=[VMEM],
        out_specs=VMEM,
        scratch_shapes=[
            pltpu.VMEM((2, half_a, 128), F32),
            pltpu.VMEM((4, half_a, 128), F32),
            pltpu.VMEM((half_a, 128), F32),
            pltpu.VMEM((2, quarter_b, 128), F32),
            pltpu.VMEM((4, quarter_b, 128), F32),
            pltpu.VMEM((8 * quarter_b, 128), F32),
            pltpu.VMEM((8 * quarter_b, 128), F32),
            pltpu.VMEM((2, half_a, 128), F32),
            pltpu.SemaphoreType.DMA((32,)),
            pltpu.SemaphoreType.DMA((32,)),
        ],
        compiler_params=params(collective_id=0, has_side_effects=True),
        name="sum_all",
    )(a)


def sum_times_kernel(p, out, core_in, mine, relay, arrive, own, swap, ssem, rsem):
    x, y_hi, y_lo, z, core = here()
    up = device((x + 1) % 4, y_hi, y_lo, z, core)
    down = device((x + 3) % 4, y_hi, y_lo, z, core)
    over = device(x, 1 - y_hi, y_lo, z, core)
    next_z = device(x, y_hi, y_lo, (z + 1) % 4, core)
    last_z = device(x, y_hi, y_lo, (z + 3) % 4, core)
    beside = device(x, y_hi, 1 - y_lo, z, core)
    partner = device(x, y_hi, y_lo, z, 1 - core)
    greet([up, down, over, next_z, last_z, beside, partner])
    send = Sender(ssem, rsem)
    order = [(h, (z + d) % 4) for d, h in ((2, 0), (2, 1), (1, 1), (3, 0), (1, 0), (3, 1), (0, 0), (0, 1))]
    swaps = [send(p.at[4 * h + q, 1 - core], core_in.at[4 * h + q], partner) for h, q in order]
    for copy, (h, q) in zip(swaps, order):
        m = 4 * h + q
        copy.wait_recv()
        mine[m] = p[m, core] + core_in[m]
    ring = RingSum(send, mine, lambda q, h: 4 * h + q, z, next_z, last_z, relay, arrive)
    ring.pass_on()
    for h in range(2):
        own[h] = ring.half(h)
    to_beside = send(own.at[1 - y_lo], swap, beside)
    to_beside.wait_recv()
    sens = 2 * x + y_hi
    out[sens] = own[y_lo] + swap[...]
    rows = out.shape[1]

    def at(y):
        return lambda q, h: (2 * q + y, pl.ds(h * (rows // 2), rows // 2))

    back = send(out.at[sens], out.at[sens], over)
    near = RingSpread(send, out, at(y_hi), x, up, down)
    near.pass_on()
    back.wait_recv()
    far = RingSpread(send, out, at(1 - y_hi), x, up, down)
    near.finish()
    far.pass_on()
    far.finish()
    send.finish()


def sum_times_call(p):
    rows = p.shape[2]
    block = (rows, 128)
    return pl.pallas_call(
        sum_times_kernel,
        out_shape=jax.ShapeDtypeStruct((8, *block), F32),
        in_specs=[VMEM],
        out_specs=VMEM,
        scratch_shapes=[
            pltpu.VMEM((8, *block), F32),
            pltpu.VMEM((8, *block), F32),
            pltpu.VMEM((2, *block), F32),
            pltpu.VMEM((4, *block), F32),
            pltpu.VMEM((2, *block), F32),
            pltpu.VMEM(block, F32),
            pltpu.SemaphoreType.DMA((32,)),
            pltpu.SemaphoreType.DMA((32,)),
        ],
        compiler_params=params(collective_id=1, has_side_effects=True),
        name="sum_times",
    )(p)


def finish_kernel(u, out, rows, recv, ssem, rsem):
    n = u.shape[0]
    sens, me = lax.axis_index("sens"), lax.axis_index("par")
    others = [(me + d) % n for d in range(1, n)]
    greet([(sens, j) for j in others])
    for c in range(n):
        rows[c] = jnp.broadcast_to(u[c : c + 1, :], (8, 128))
    send = Sender(ssem, rsem)
    for d, j in enumerate(others):
        send(rows.at[j], recv.at[d], (sens, j))
    total = rows[me]
    for d, copy in enumerate(send.sent):
        copy.wait_recv()
        total = total + recv[d]
    out[...] = total[0:1, 0 : out.shape[1]]
    send.finish()


def finish_call(u, width):
    n = u.shape[0]
    return pl.pallas_call(
        finish_kernel,
        out_shape=jax.ShapeDtypeStruct((1, width), F32),
        in_specs=[VMEM],
        out_specs=VMEM,
        scratch_shapes=[
            pltpu.VMEM((n, 8, 128), F32),
            pltpu.VMEM((n - 1, 8, 128), F32),
            pltpu.SemaphoreType.DMA((n - 1,)),
            pltpu.SemaphoreType.DMA((n - 1,)),
        ],
        compiler_params=params(collective_id=2, has_side_effects=True),
        name="finish",
    )(u)


def shards(records, spec_real, spec_imag, prior_cov, sensor_map, inverse_rows):
    tabs = tables()
    sr, si = spec_real.transpose(1, 0, 2), spec_imag.transpose(1, 0, 2)
    place = (sensor_map // SD * 128 + sensor_map % SD).astype(jnp.int32)[None]
    a = adjoint_call(records.transpose(1, 0, 2), sr, si, tabs)
    a = sum_all_call(a.reshape(COLS * NT, PD)).reshape(COLS, NT, PD)
    p = forward_call(a, prior_cov, sr, si, tabs)
    g = sum_times_call(p.reshape(8, 2, NT, 128))
    u = update_call(place, g, inverse_rows.transpose(1, 0, 2))
    return finish_call(u, inverse_rows.shape[0])


def solution(mesh):
    return jax.shard_map(
        shards,
        mesh=mesh,
        in_specs=(
            P(None, "sens", None),
            P(None, "sens", "par"),
            P(None, "sens", "par"),
            P(),
            P(),
            P("sens", "par", None),
        ),
        out_specs=P("par", "sens"),
        check_vma=False,
    )
```

```python
import functools
import math

import jax
import jax.numpy as jnp
import ml_dtypes
import numpy as np
from jax import lax
from jax.experimental import pallas as pl
from jax.experimental.pallas import tpu as pltpu
from jax.sharding import PartitionSpec as P

MESH = pl.DeviceIdType.MESH
F32, BF16 = jnp.float32, jnp.bfloat16
VMEM = pl.BlockSpec(memory_space=pltpu.VMEM)
ANY = pl.BlockSpec(memory_space=pl.ANY)
HBM = pl.BlockSpec(memory_space=pltpu.HBM)

COLS, NT, NF = 16, 224, 225
SD, PD = 75, 128
SPAD = 80
FR = 232
ROWS2 = 2 * COLS
CHUNK = 25
NCHUNK = NF // CHUNK
UNROLL = 25
BLOCKS, STEPS, SPADT = 16, 14, 16
GROUP = 8
WIDE = GROUP * SPAD
HALVES = 2
HALF_ROWS = COLS * NT // HALVES
HALF_A, QUARTER_B = 128, 48
NT_DIMS = ((1,), (1,))
LIMIT = 60 * 2**20


def split_np(table):
    high = table.astype(np.float32).astype(ml_dtypes.bfloat16)
    low = (table - high.astype(np.float64)).astype(np.float32).astype(ml_dtypes.bfloat16)
    return high, low


def thrice_np(table):
    pieces = []
    for at in range(0, table.shape[1], 256):
        high, low = split_np(table[:, at : at + 256])
        pieces += [high, low, high]
    return np.concatenate(pieces, axis=1)


def tables():
    length = 2 * NT
    w = np.arange(NF)
    t = np.arange(NT)
    phase = (np.outer(w, t) % length) * (2.0 * math.pi / length)
    fwd = np.zeros((2 * FR, 256))
    fwd[:NF, :NT] = np.cos(phase)
    fwd[FR : FR + NF, :NT] = -np.sin(phase)
    weight = np.where((w == 0) | (w == NT), 1.0, 2.0) / length
    inv = np.zeros((NT, 512))
    inv[:, :NF] = np.cos(phase).T * weight
    inv[:, 256 : 256 + NF] = -np.sin(phase).T * weight
    blocks = np.zeros((BLOCKS, SPADT, 512))
    blocks[:, :STEPS] = inv.reshape(BLOCKS, STEPS, 512)
    return tuple(thrice_np(table) for table in (fwd, inv, blocks.reshape(-1, 512)))


def split(x):
    high = x.astype(BF16)
    return high, (x - high.astype(F32)).astype(BF16)


def dot(a, b, dims=((1,), (0,))):
    return lax.dot_general(a, b, (dims, ((), ())), preferred_element_type=F32)


def thrice(x, axis):
    high, low = split(x)
    return [jnp.concatenate([high, high, low], axis=axis)]


def dot3(a, b, dims=((1,), (0,))):
    return dot(a[0], b[0], dims) + (dot(a[1], b[0], dims) + dot(a[0], b[1], dims))


def here():
    sens, par = lax.axis_index("sens"), lax.axis_index("par")
    return sens // 2, sens % 2, par // 8, par // 2 % 4, par % 2


def device(x, y_hi, y_lo, z, core):
    return (x * 2 + y_hi, y_lo * 8 + z * 2 + core)


def greet(devices):
    barrier = pltpu.get_barrier_semaphore()
    for d in devices:
        pl.semaphore_signal(barrier, inc=1, device_id=d, device_id_type=MESH)


def all_here(devices):
    pl.semaphore_wait(pltpu.get_barrier_semaphore(), len(devices))


class Sender:
    def __init__(self, send_sems, recv_sems):
        self.send_sems, self.recv_sems, self.sent = send_sems, recv_sems, []

    def __call__(self, src, dst, to):
        k = len(self.sent)
        copy = pltpu.make_async_remote_copy(
            src_ref=src,
            dst_ref=dst,
            send_sem=self.send_sems.at[k],
            recv_sem=self.recv_sems.at[k],
            device_id=to,
            device_id_type=MESH,
        )
        copy.start()
        self.sent.append(copy)
        return copy

    def finish(self):
        for copy in self.sent:
            copy.wait_send()


def rows_at(start, size):
    return pl.ds(pl.multiple_of(start, 8), size)


class RingSum:
    def __init__(self, send, data, at, place, up, down, relay, arrive):
        self.send, self.data, self.at, self.place = send, data, at, place
        self.up, self.down, self.relay, self.arrive = up, down, relay, arrive
        nxt, prv, far = (place + 1) % 4, (place + 3) % 4, (place + 2) % 4
        self.nxt, self.prv = nxt, prv
        self.far_up = send(data.at[at(far, 0)], relay.at[0], up)
        self.far_down = send(data.at[at(far, 1)], relay.at[1], down)
        self.near_up = send(data.at[at(nxt, 1)], arrive.at[0], up)
        self.near_down = send(data.at[at(prv, 0)], arrive.at[1], down)

    def pass_on(self):
        self.far_up.wait_recv()
        self.relay[0] = self.relay[0] + self.data[self.at(self.nxt, 0)]
        self.last_up = self.send(self.relay.at[0], self.arrive.at[2], self.up)
        self.far_down.wait_recv()
        self.relay[1] = self.relay[1] + self.data[self.at(self.prv, 1)]
        self.last_down = self.send(self.relay.at[1], self.arrive.at[3], self.down)

    def half(self, h):
        (self.near_down, self.near_up)[h].wait_recv()
        (self.last_up, self.last_down)[h].wait_recv()
        own = self.data[self.at(self.place, h)]
        return own + self.arrive[(1, 0)[h]] + self.arrive[(2, 3)[h]]


class RingSpread:
    def __init__(self, send, data, at, place, up, down):
        self.send, self.data, self.at, self.place, self.up, self.down = send, data, at, place, up, down
        mine = [data.at[at(place, h)] for h in range(2)]
        self.first_up = send(mine[0], mine[0], up)
        self.first_down = send(mine[1], mine[1], down)
        self.second_up = send(mine[1], mine[1], up)
        self.second_down = send(mine[0], mine[0], down)

    def pass_on(self):
        self.first_up.wait_recv()
        piece = self.data.at[self.at((self.place + 3) % 4, 0)]
        self.far_up = self.send(piece, piece, self.up)
        self.first_down.wait_recv()
        piece = self.data.at[self.at((self.place + 1) % 4, 1)]
        self.far_down = self.send(piece, piece, self.down)

    def finish(self):
        for copy in (self.second_up, self.second_down, self.far_up, self.far_down):
            copy.wait_recv()


PEERS = ((1, 2), (0, 2), (1, 1), (1, 3), (1, 0), (0, 1), (0, 3))


class Refs:
    def __init__(self, names, refs):
        for name, ref in zip(names, refs, strict=True):
            setattr(self, name, ref)


def start_specs(r):
    @pl.loop(0, SD)
    def _(s):
        pltpu.make_async_copy(r.sr_hbm.at[s], r.sr.at[:, s, :], r.spec_sem.at[0]).start()
        pltpu.make_async_copy(r.si_hbm.at[s], r.si.at[:, s, :], r.spec_sem.at[1]).start()

    blank = jnp.zeros((CHUNK, SPAD - SD, PD), F32)

    @pl.loop(0, NCHUNK)
    def _(i):
        r.sr[pl.ds(i * CHUNK, CHUNK), SD:SPAD, :] = blank
        r.si[pl.ds(i * CHUNK, CHUNK), SD:SPAD, :] = blank


def wait_specs(r):
    @pl.loop(0, SD)
    def _(s):
        pltpu.make_async_copy(r.sr_hbm.at[s], r.sr.at[:, s, :], r.spec_sem.at[0]).wait()
        pltpu.make_async_copy(r.si_hbm.at[s], r.si.at[:, s, :], r.spec_sem.at[1]).wait()


def part_rows(c):
    return (c, COLS + c)


def pair_rows(q):
    return [row for half in range(2) for row in part_rows(2 * q + half)]


def out_row(r, row, q):
    return pltpu.make_async_copy(r.xn.at[row, pl.ds(0, NF)], r.rows_hbm.at[row], r.xsem.at[0, q])


def in_row(r, row, q):
    return pltpu.make_async_copy(r.rows_hbm.at[row], r.x.at[:, row, :], r.xsem.at[1, q])


def put_spectrum(r, res, q):
    for half in range(2):
        for part, row in enumerate(part_rows(2 * q + half)):
            r.xn[row, 0:FR, :] = res[part * FR : (part + 1) * FR, half * 128 : (half + 1) * 128]
            out_row(r, row, q).start()


def turn_rows(r, q):
    for row in pair_rows(q):
        out_row(r, row, q).wait()
    for row in pair_rows(q):
        in_row(r, row, q).start()


def spectra(r, first, last, pair_of, table, dims):
    @pl.loop(first, last)
    def _(q):
        both = thrice(pair_of(q), dims[1][0])[0]
        put_spectrum(r, dot(table[...], both, dims), q)

        @pl.when(q > first)
        def _():
            turn_rows(r, q - 1)


def wait_spectra(r):
    @pl.loop(0, COLS // 2)
    def _(q):
        for row in pair_rows(q):
            in_row(r, row, q).wait()

    @pl.loop(0, ROWS2)
    def _(row):
        r.xn[row, NF:256, :] = jnp.zeros((256 - NF, 128), F32)


def out_chunk(r, i):
    at = pl.ds(i * CHUNK, CHUNK)
    return pltpu.make_async_copy(r.y.at[at], r.freq_hbm.at[at], r.ysem.at[i])


def in_column(r, row, q):
    return pltpu.make_async_copy(r.freq_hbm.at[:, row, :], r.xn.at[row, pl.ds(0, NF)], r.csem.at[q])


def over_frequencies(r, step):
    @pl.loop(0, NCHUNK)
    def _(i):
        @pl.loop(0, CHUNK // UNROLL)
        def _(j):
            for u in range(UNROLL):
                step(i * CHUNK + j * UNROLL + u)

        out_chunk(r, i).start()

    @pl.loop(0, NCHUNK)
    def _(i):
        out_chunk(r, i).wait()

    @pl.loop(0, COLS // 2)
    def _(q):
        for row in pair_rows(q):
            in_column(r, row, q).start()


def wait_columns(r, q):
    for row in pair_rows(q):
        in_column(r, row, q).wait()


def to_samples(columns, table):
    both = jnp.concatenate(thrice(columns(0), 0) + thrice(columns(1), 0), axis=0)
    return dot(table[...], both)


def record_pairs(r):
    flat, rec = r.flat, r.rec
    flat[0] = r.rec_in[:, :, 0:128]
    flat[1, :, :, 0 : NT - 128] = r.rec_in[:, :, 128:NT]
    flat[1, :, :, NT - 128 : 128] = jnp.zeros((SD, COLS, 256 - NT), F32)

    def row_copy(side, c):
        return pltpu.make_async_copy(
            flat.at[side, :, c, :], rec.at[side, c, pl.ds(0, SD)], r.rsem.at[side]
        )

    @pl.loop(0, COLS)
    def _(c):
        row_copy(0, c).start()
        row_copy(1, c).start()
        rec[0, c, SD:128, :] = jnp.zeros((128 - SD, 128), F32)
        rec[1, c, SD:128, :] = jnp.zeros((128 - SD, 128), F32)

    @pl.loop(0, COLS)
    def _(c):
        row_copy(0, c).wait()
        row_copy(1, c).wait()

    def pair_of(q):
        sides = [rec[side, pl.ds(2 * q, 2)].reshape(256, 128) for side in range(2)]
        return jnp.concatenate(sides, axis=1)

    return pair_of


def adjoint_spectrum(r):
    start_specs(r)
    spectra(r, 0, COLS // 2, record_pairs(r), r.forward_table, NT_DIMS)
    turn_rows(r, COLS // 2 - 1)
    wait_spectra(r)
    wait_specs(r)

    def step(w):
        ah, al = split(r.x[w][:, :SPAD])
        both = split(jnp.concatenate([r.sr[w], r.si[w]], axis=1))
        wide = dot(jnp.concatenate([ah, al], axis=0), both[0])
        p = wide[:ROWS2] + (wide[ROWS2:] + dot(ah, both[1]))
        r.y[w] = jnp.concatenate(
            [p[:COLS, :PD] + p[COLS:, PD:], p[COLS:, :PD] - p[:COLS, PD:]], axis=0
        )

    over_frequencies(r, step)


def adjoint_samples(r, first, last):
    @pl.loop(first, last)
    def _(q):
        wait_columns(r, q)
        res = to_samples(
            lambda part: jnp.concatenate(
                [r.xn[part * COLS + 2 * q], r.xn[part * COLS + 2 * q + 1]], axis=1
            ),
            r.inverse_table,
        )
        r.adj[2 * q] = res[:, :PD]
        r.adj[2 * q + 1] = res[:, PD:]


def weighted_table(r):
    table = r.forward_table
    high, low = split(dot3((table[:, 0:NT], table[:, 256 : 256 + NT]), split(r.prior[...])))
    r.weighted[...] = jnp.zeros_like(r.weighted)
    for i, piece in enumerate((high, low, high)):
        r.weighted[:, 256 * i : 256 * i + NT] = piece


def field_spectra(r, first, last):
    def pair_of(q):
        pair = jnp.concatenate([r.all_adj[2 * q], r.all_adj[2 * q + 1]], axis=1)
        return jnp.concatenate([pair, jnp.zeros((256 - NT, 256), F32)], axis=0)

    spectra(r, first, last, pair_of, r.weighted, ((1,), (0,)))
    turn_rows(r, last - 1)


def predicted_spectrum(r):
    wait_spectra(r)

    def step(w):
        f = r.x[w]
        re, im = f[:COLS], f[COLS:]
        fh, fl = split(f)
        left = jnp.concatenate(
            [jnp.concatenate([fh, fh], axis=1), jnp.concatenate([fl, jnp.zeros_like(fl)], axis=1)],
            axis=0,
        )
        prods = []
        for s in (r.sr, r.si):
            wide = dot(left, jnp.concatenate(split(s[w]), axis=1), NT_DIMS)
            prods.append(wide[:ROWS2] + wide[ROWS2:])
        p, q = prods
        r.y[w, :, 0:SPAD] = jnp.concatenate([p[:COLS] - q[COLS:], p[COLS:] + q[:COLS]], axis=0)

    over_frequencies(r, step)


def predicted_samples(r, g):
    for k in range(GROUP // 2):
        wait_columns(r, g * GROUP // 2 + k)
    res = to_samples(
        lambda part: jnp.concatenate(
            [r.xn[part * COLS + g * GROUP + k][:, :SPAD] for k in range(GROUP)], axis=1
        ),
        r.block_table,
    )
    r.p[g] = res.reshape(8, 2, SPADT, WIDE)


def selection(r):
    keys = r.pick.shape[1]

    @pl.loop(0, 8)
    def _(i):
        at = pl.ds(pl.multiple_of(i * SPAD, SPAD), SPAD)
        row = lax.broadcasted_iota(jnp.int32, (SPAD, keys), 0)
        chosen = (row + i * SD == r.place[...]) & (row < SD)
        r.pick[at, :] = chosen.astype(F32).astype(BF16)


def split_inverse(r):
    @pl.loop(0, STEPS)
    def _(t):
        high, low = split(r.inv[t])
        r.ih[t] = high
        r.il[t] = low


def put_in_order(r, g):
    left = jnp.concatenate(
        [
            jnp.concatenate([r.gath[g, i][:, k * SPAD : (k + 1) * SPAD] for i in range(8)], axis=1)
            for k in range(GROUP)
        ],
        axis=0,
    )
    high, low = split(left)
    res = dot(high, r.pick[...]) + dot(low, r.pick[...])
    for k in range(GROUP):
        r.perm[:, g * GROUP + k, :] = res[k * SPADT : (k + 1) * SPADT, :]


def apply_inverse(r):
    rows = r.ih.shape[1]
    r.u[...] = jnp.zeros_like(r.u)

    @pl.loop(0, STEPS)
    def _(t):
        r.u[:, 0:rows] += dot3(split(r.perm[t]), (r.ih[t], r.il[t]), NT_DIMS)


def sum_all(r, send, half, place, up, down, over):
    x, y_hi = place
    start = half * HALF_ROWS
    start_b = start + 8 * HALF_A
    size_b = 8 * QUARTER_B
    a, out = r.adj_rows, r.all_rows
    swap_a, swap_b, half_b, done_a = (
        ref.at[half] for ref in (r.swap_a, r.swap_b, r.half_b, r.done_a)
    )

    def at_a(q, h):
        return rows_at(start + (2 * q + h) * HALF_A, HALF_A)

    def at_half_b(q, h):
        return rows_at((2 * q + h) * QUARTER_B, QUARTER_B)

    def place_b(q, h):
        return rows_at(start_b + y_hi * size_b + (2 * q + h) * QUARTER_B, QUARTER_B)

    theirs = rows_at(start_b + (1 - y_hi) * size_b, size_b)
    ours = rows_at(start_b + y_hi * size_b, size_b)
    to_over_b = send(a.at[theirs], swap_b, over)
    ring_a = RingSum(send, a, at_a, x, up, down, r.relay_a.at[half], r.arrive_a.at[half])
    yield
    ring_a.pass_on()
    to_over_b.wait_recv()
    half_b[...] = a[ours] + swap_b[...]
    ring_b = RingSum(send, half_b, at_half_b, x, up, down, r.relay_b.at[half], r.arrive_b.at[half])
    yield
    for h in range(2):
        done_a[h] = ring_a.half(h)
    to_over_a = send(done_a.at[1 - y_hi], swap_a, over)
    ring_b.pass_on()
    yield
    to_over_a.wait_recv()
    mine = at_a(x, y_hi)
    out[mine] = done_a[y_hi] + swap_a[...]
    back_a = send(out.at[mine], out.at[mine], over)
    for h in range(2):
        out[place_b(x, h)] = ring_b.half(h)
    spread_b = RingSpread(send, out, place_b, x, up, down)
    yield
    back_a.wait_recv()
    spread_a = RingSpread(send, out, at_a, x, up, down)
    spread_b.pass_on()
    yield
    spread_b.finish()
    back_b = send(out.at[ours], out.at[ours], over)
    spread_a.pass_on()
    yield
    spread_a.finish()
    back_b.wait_recv()
    yield


def sum_times(r, send, g, place, links):
    x, y_hi, y_lo, z, core = place
    next_z, last_z, beside, partner = links[:4]
    p, core_in, mine, own, swap, out = (
        ref.at[g] for ref in (r.p, r.core_in, r.mine, r.own, r.swap_t, r.gath)
    )
    order = [(h, (z + d) % 4) for d, h in ((2, 0), (2, 1), (1, 1), (3, 0), (1, 0), (3, 1), (0, 0), (0, 1))]
    swaps = [send(p.at[4 * h + q, 1 - core], core_in.at[4 * h + q], partner) for h, q in order]
    yield
    for copy, (h, q) in zip(swaps, order):
        m = 4 * h + q
        copy.wait_recv()
        mine[m] = p[m, core] + core_in[m]
    ring = RingSum(
        send, mine, lambda q, h: 4 * h + q, z, next_z, last_z, r.relay_t.at[g], r.arrive_t.at[g]
    )
    yield
    ring.pass_on()
    yield
    for h in range(2):
        own[h] = ring.half(h)
    to_beside = send(own.at[1 - y_lo], swap, beside)
    yield
    to_beside.wait_recv()
    sens = 2 * x + y_hi
    out[sens] = own[y_lo] + swap[...]

    copies = [send(out.at[sens], out.at[sens], to) for to in links[4:]]
    yield
    for copy in copies:
        copy.wait_recv()
    yield


def finish(r, send, others, sens, me):
    for c in range(COLS):
        r.rows[c] = jnp.broadcast_to(r.u[c : c + 1, :], (8, 128))
    sent = [send(r.rows.at[j], r.recv.at[d], (sens, j)) for d, j in enumerate(others)]
    total = r.rows[me]
    for d, copy in enumerate(sent):
        copy.wait_recv()
        total = total + r.recv[d]
    r.out[...] = total[0:1, 0 : r.out.shape[1]]


INPUTS = [
    "rec_in",
    "sr_hbm",
    "si_hbm",
    "prior",
    "place",
    "inv_hbm",
    "forward_table",
    "inverse_table",
    "block_table",
]
OUTPUTS = ["out", "rows_hbm", "freq_hbm"]


def scratch(keys, rows):
    dma = pltpu.SemaphoreType.DMA
    part = (HALVES,)
    t_block = (SPADT, WIDE)
    messages = 150
    return dict(
        sr=pltpu.VMEM((NF, SPAD, PD), F32),
        si=pltpu.VMEM((NF, SPAD, PD), F32),
        x=pltpu.VMEM((NF, ROWS2, 128), F32),
        y=pltpu.VMEM((NF, ROWS2, 128), F32),
        xn=pltpu.VMEM((ROWS2, 256, 128), F32),
        flat=pltpu.VMEM((2, SD, COLS, 128), F32),
        rec=pltpu.VMEM((2, COLS, 128, 128), F32),
        adj=pltpu.VMEM((COLS, NT, PD), F32),
        all_adj=pltpu.VMEM((COLS, NT, PD), F32),
        weighted=pltpu.VMEM((2 * FR, 768), BF16),
        relay_a=pltpu.VMEM((*part, 2, HALF_A, 128), F32),
        arrive_a=pltpu.VMEM((*part, 4, HALF_A, 128), F32),
        swap_a=pltpu.VMEM((*part, HALF_A, 128), F32),
        done_a=pltpu.VMEM((*part, 2, HALF_A, 128), F32),
        relay_b=pltpu.VMEM((*part, 2, QUARTER_B, 128), F32),
        arrive_b=pltpu.VMEM((*part, 4, QUARTER_B, 128), F32),
        swap_b=pltpu.VMEM((*part, 8 * QUARTER_B, 128), F32),
        half_b=pltpu.VMEM((*part, 8 * QUARTER_B, 128), F32),
        p=pltpu.VMEM((*part, 8, 2, *t_block), F32),
        core_in=pltpu.VMEM((*part, 8, *t_block), F32),
        mine=pltpu.VMEM((*part, 8, *t_block), F32),
        relay_t=pltpu.VMEM((*part, 2, *t_block), F32),
        arrive_t=pltpu.VMEM((*part, 4, *t_block), F32),
        own=pltpu.VMEM((*part, 2, *t_block), F32),
        swap_t=pltpu.VMEM((*part, *t_block), F32),
        gath=pltpu.VMEM((*part, 8, *t_block), F32),
        pick=pltpu.VMEM((8 * SPAD, keys), BF16),
        inv=pltpu.VMEM((STEPS, rows, keys), F32),
        ih=pltpu.VMEM((STEPS, rows, keys), BF16),
        il=pltpu.VMEM((STEPS, rows, keys), BF16),
        perm=pltpu.VMEM((SPADT, COLS, keys), F32),
        u=pltpu.VMEM((COLS, 128), F32),
        rows=pltpu.VMEM((COLS, 8, 128), F32),
        recv=pltpu.VMEM((COLS - 1, 8, 128), F32),
        spec_sem=dma((2,)),
        rsem=dma((2,)),
        xsem=dma((2, COLS // 2)),
        ysem=dma((NCHUNK,)),
        csem=dma((COLS // 2,)),
        inv_sem=dma,
        ssem=dma((messages,)),
        msem=dma((messages,)),
    )


def kernel(names, *refs):
    r = Refs(names, refs)
    r.adj_rows = r.adj.reshape(COLS * NT, PD)
    r.all_rows = r.all_adj.reshape(COLS * NT, PD)
    x, y_hi, y_lo, z, core = place = here()
    sens, me = lax.axis_index("sens"), lax.axis_index("par")
    up = device((x + 1) % 4, y_hi, y_lo, z, core)
    down = device((x + 3) % 4, y_hi, y_lo, z, core)
    over = device(x, 1 - y_hi, y_lo, z, core)
    next_z = device(x, y_hi, y_lo, (z + 1) % 4, core)
    last_z = device(x, y_hi, y_lo, (z + 3) % 4, core)
    beside = device(x, y_hi, 1 - y_lo, z, core)
    partner = device(x, y_hi, y_lo, z, 1 - core)
    others = [(me + d) % COLS for d in range(1, COLS)]
    friends = [(sens, j) for j in others]
    around = [device((x + d) % 4, (y_hi + e) % 2, y_lo, z, core) for e, d in PEERS]
    friends += around
    links = (next_z, last_z, beside, partner, *around)
    greet(friends)
    send = Sender(r.ssem, r.msem)
    adjoint_spectrum(r)
    inverse = pltpu.make_async_copy(r.inv_hbm, r.inv, r.inv_sem)
    inverse.start()
    pairs = COLS // 2 // HALVES
    adjoint_samples(r, 0, pairs)
    all_here(friends)
    first = sum_all(r, send, 0, (x, y_hi), up, down, over)
    next(first)
    adjoint_samples(r, pairs, 2 * pairs)
    second = sum_all(r, send, 1, (x, y_hi), up, down, over)
    next(second)
    weighted_table(r)
    for _ in range(4):
        next(first)
        next(second)
    selection(r)
    next(first)
    next(second)
    next(first)
    field_spectra(r, 0, pairs)
    next(second)
    field_spectra(r, pairs, 2 * pairs)
    predicted_spectrum(r)
    predicted_samples(r, 0)
    first = sum_times(r, send, 0, place, links)
    next(first)
    predicted_samples(r, 1)
    second = sum_times(r, send, 1, place, links)
    next(second)
    inverse.wait()
    for step in range(3):
        next(first)
        next(second)
    split_inverse(r)
    for step in range(1):
        next(first)
        next(second)
    next(first)
    put_in_order(r, 0)
    next(second)
    put_in_order(r, 1)
    apply_inverse(r)
    finish(r, send, others, sens, me)
    send.finish()


def shards(records, spec_real, spec_imag, prior_cov, sensor_map, inverse_rows):
    tabs = tables()
    sr, si = spec_real.transpose(1, 0, 2), spec_imag.transpose(1, 0, 2)
    place = sensor_map[None]
    rows, _, keys = inverse_rows.shape
    spaces = scratch(keys, rows)
    out, _, _ = pl.pallas_call(
        functools.partial(kernel, INPUTS + OUTPUTS + list(spaces)),
        out_shape=(
            jax.ShapeDtypeStruct((1, rows), F32),
            jax.ShapeDtypeStruct((ROWS2, NF, 128), F32),
            jax.ShapeDtypeStruct((NF, ROWS2, 128), F32),
        ),
        in_specs=[VMEM, ANY, ANY, VMEM, VMEM, ANY] + [VMEM] * 3,
        out_specs=(VMEM, HBM, HBM),
        scratch_shapes=list(spaces.values()),
        compiler_params=pltpu.CompilerParams(
            vmem_limit_bytes=LIMIT, collective_id=0, has_side_effects=True
        ),
        name="tsunami",
    )(records.transpose(1, 0, 2), sr, si, prior_cov, place, inverse_rows.transpose(1, 0, 2), *tabs)
    return out


def solution(mesh):
    return jax.shard_map(
        shards,
        mesh=mesh,
        in_specs=(
            P(None, "sens", None),
            P(None, "sens", "par"),
            P(None, "sens", "par"),
            P(),
            P(),
            P("sens", "par", None),
        ),
        out_specs=P("par", "sens"),
        check_vma=False,
    )
```

```python
import functools
import math

import jax
import jax.numpy as jnp
import ml_dtypes
import numpy as np
from jax import lax
from jax.experimental import pallas as pl
from jax.experimental.pallas import tpu as pltpu
from jax.sharding import PartitionSpec as P

MESH = pl.DeviceIdType.MESH
F32, BF16 = jnp.float32, jnp.bfloat16
VMEM = pl.BlockSpec(memory_space=pltpu.VMEM)
ANY = pl.BlockSpec(memory_space=pl.ANY)
HBM = pl.BlockSpec(memory_space=pltpu.HBM)

COLS, NT, NF = 16, 224, 225
SD, PD = 75, 128
SPAD = 80
FR = 232
ROWS2 = 2 * COLS
CHUNK = 25
NCHUNK = NF // CHUNK
UNROLL = 25
BLOCKS, STEPS, SPADT = 16, 14, 16
GROUP = 8
WIDE = GROUP * SPAD
HALVES = 2
HALF_ROWS = COLS * NT // HALVES
HALF_A, QUARTER_B = 128, 48
NT_DIMS = ((1,), (1,))
LIMIT = 60 * 2**20


def split_np(table):
    high = table.astype(np.float32).astype(ml_dtypes.bfloat16)
    low = (table - high.astype(np.float64)).astype(np.float32).astype(ml_dtypes.bfloat16)
    return high, low


def thrice_np(table):
    pieces = []
    for at in range(0, table.shape[1], 256):
        high, low = split_np(table[:, at : at + 256])
        pieces += [high, low, high]
    return np.concatenate(pieces, axis=1)


def tables():
    length = 2 * NT
    w = np.arange(NF)
    t = np.arange(NT)
    phase = (np.outer(w, t) % length) * (2.0 * math.pi / length)
    fwd = np.zeros((2 * FR, 256))
    fwd[:NF, :NT] = np.cos(phase)
    fwd[FR : FR + NF, :NT] = -np.sin(phase)
    weight = np.where((w == 0) | (w == NT), 1.0, 2.0) / length
    inv = np.zeros((NT, 512))
    inv[:, :NF] = np.cos(phase).T * weight
    inv[:, 256 : 256 + NF] = -np.sin(phase).T * weight
    blocks = np.zeros((BLOCKS, SPADT, 512))
    blocks[:, :STEPS] = inv.reshape(BLOCKS, STEPS, 512)
    return tuple(thrice_np(table) for table in (fwd, inv, blocks.reshape(-1, 512)))


def split(x):
    high = x.astype(BF16)
    return high, (x - high.astype(F32)).astype(BF16)


def dot(a, b, dims=((1,), (0,))):
    return lax.dot_general(a, b, (dims, ((), ())), preferred_element_type=F32)


def thrice(x, axis):
    high, low = split(x)
    return [jnp.concatenate([high, high, low], axis=axis)]


def dot3(a, b, dims=((1,), (0,))):
    return dot(a[0], b[0], dims) + (dot(a[1], b[0], dims) + dot(a[0], b[1], dims))


def here():
    sens, par = lax.axis_index("sens"), lax.axis_index("par")
    return sens // 2, sens % 2, par // 8, par // 2 % 4, par % 2


def device(x, y_hi, y_lo, z, core):
    return (x * 2 + y_hi, y_lo * 8 + z * 2 + core)


def greet(devices):
    barrier = pltpu.get_barrier_semaphore()
    for d in devices:
        pl.semaphore_signal(barrier, inc=1, device_id=d, device_id_type=MESH)


def all_here(devices):
    pl.semaphore_wait(pltpu.get_barrier_semaphore(), len(devices))


class Sender:
    def __init__(self, send_sems, recv_sems):
        self.send_sems, self.recv_sems, self.sent = send_sems, recv_sems, []

    def __call__(self, src, dst, to):
        k = len(self.sent)
        copy = pltpu.make_async_remote_copy(
            src_ref=src,
            dst_ref=dst,
            send_sem=self.send_sems.at[k],
            recv_sem=self.recv_sems.at[k],
            device_id=to,
            device_id_type=MESH,
        )
        copy.start()
        self.sent.append(copy)
        return copy

    def finish(self):
        for copy in self.sent:
            copy.wait_send()


def rows_at(start, size):
    return pl.ds(pl.multiple_of(start, 8), size)


class RingSum:
    def __init__(self, send, data, at, place, up, down, relay, arrive):
        self.send, self.data, self.at, self.place = send, data, at, place
        self.up, self.down, self.relay, self.arrive = up, down, relay, arrive
        nxt, prv, far = (place + 1) % 4, (place + 3) % 4, (place + 2) % 4
        self.nxt, self.prv = nxt, prv
        self.far_up = send(data.at[at(far, 0)], relay.at[0], up)
        self.far_down = send(data.at[at(far, 1)], relay.at[1], down)
        self.near_up = send(data.at[at(nxt, 1)], arrive.at[0], up)
        self.near_down = send(data.at[at(prv, 0)], arrive.at[1], down)

    def pass_on(self):
        self.far_up.wait_recv()
        self.relay[0] = self.relay[0] + self.data[self.at(self.nxt, 0)]
        self.last_up = self.send(self.relay.at[0], self.arrive.at[2], self.up)
        self.far_down.wait_recv()
        self.relay[1] = self.relay[1] + self.data[self.at(self.prv, 1)]
        self.last_down = self.send(self.relay.at[1], self.arrive.at[3], self.down)

    def half(self, h):
        (self.near_down, self.near_up)[h].wait_recv()
        (self.last_up, self.last_down)[h].wait_recv()
        own = self.data[self.at(self.place, h)]
        return own + self.arrive[(1, 0)[h]] + self.arrive[(2, 3)[h]]


class RingSpread:
    def __init__(self, send, data, at, place, up, down):
        self.send, self.data, self.at, self.place, self.up, self.down = send, data, at, place, up, down
        mine = [data.at[at(place, h)] for h in range(2)]
        self.first_up = send(mine[0], mine[0], up)
        self.first_down = send(mine[1], mine[1], down)
        self.second_up = send(mine[1], mine[1], up)
        self.second_down = send(mine[0], mine[0], down)

    def pass_on(self):
        self.first_up.wait_recv()
        piece = self.data.at[self.at((self.place + 3) % 4, 0)]
        self.far_up = self.send(piece, piece, self.up)
        self.first_down.wait_recv()
        piece = self.data.at[self.at((self.place + 1) % 4, 1)]
        self.far_down = self.send(piece, piece, self.down)

    def finish(self):
        for copy in (self.second_up, self.second_down, self.far_up, self.far_down):
            copy.wait_recv()


PEERS = ((1, 2), (0, 2), (1, 1), (1, 3), (1, 0), (0, 1), (0, 3))


class Refs:
    def __init__(self, names, refs):
        for name, ref in zip(names, refs, strict=True):
            setattr(self, name, ref)


def start_specs(r):
    @pl.loop(0, SD)
    def _(s):
        pltpu.make_async_copy(r.sr_hbm.at[s], r.sr.at[:, s, :], r.spec_sem.at[0]).start()
        pltpu.make_async_copy(r.si_hbm.at[s], r.si.at[:, s, :], r.spec_sem.at[1]).start()

    blank = jnp.zeros((CHUNK, SPAD - SD, PD), F32)

    @pl.loop(0, NCHUNK)
    def _(i):
        r.sr[pl.ds(i * CHUNK, CHUNK), SD:SPAD, :] = blank
        r.si[pl.ds(i * CHUNK, CHUNK), SD:SPAD, :] = blank


def wait_specs(r):
    @pl.loop(0, SD)
    def _(s):
        pltpu.make_async_copy(r.sr_hbm.at[s], r.sr.at[:, s, :], r.spec_sem.at[0]).wait()
        pltpu.make_async_copy(r.si_hbm.at[s], r.si.at[:, s, :], r.spec_sem.at[1]).wait()


def part_rows(c):
    return (c, COLS + c)


def pair_rows(q):
    return [row for half in range(2) for row in part_rows(2 * q + half)]


def out_row(r, row, q):
    return pltpu.make_async_copy(r.xn.at[row, pl.ds(0, NF)], r.rows_hbm.at[row], r.xsem.at[0, q])


def in_row(r, row, q):
    return pltpu.make_async_copy(r.rows_hbm.at[row], r.x.at[:, row, :], r.xsem.at[1, q])


def put_spectrum(r, res, q):
    for half in range(2):
        for part, row in enumerate(part_rows(2 * q + half)):
            r.xn[row, 0:FR, :] = res[part * FR : (part + 1) * FR, half * 128 : (half + 1) * 128]
            out_row(r, row, q).start()


def turn_rows(r, q):
    for row in pair_rows(q):
        out_row(r, row, q).wait()
    for row in pair_rows(q):
        in_row(r, row, q).start()


def spectra(r, first, last, pair_of, table, dims):
    @pl.loop(first, last)
    def _(q):
        both = thrice(pair_of(q), dims[1][0])[0]
        put_spectrum(r, dot(table[...], both, dims), q)

        @pl.when(q > first)
        def _():
            turn_rows(r, q - 1)


def wait_spectra(r):
    @pl.loop(0, COLS // 2)
    def _(q):
        for row in pair_rows(q):
            in_row(r, row, q).wait()

    @pl.loop(0, ROWS2)
    def _(row):
        r.xn[row, NF:256, :] = jnp.zeros((256 - NF, 128), F32)


def out_chunk(r, i):
    at = pl.ds(i * CHUNK, CHUNK)
    return pltpu.make_async_copy(r.y.at[at], r.freq_hbm.at[at], r.ysem.at[i])


def in_column(r, row, q):
    return pltpu.make_async_copy(r.freq_hbm.at[:, row, :], r.xn.at[row, pl.ds(0, NF)], r.csem.at[q])


def over_frequencies(r, step):
    @pl.loop(0, NCHUNK)
    def _(i):
        @pl.loop(0, CHUNK // UNROLL)
        def _(j):
            for u in range(UNROLL):
                step(i * CHUNK + j * UNROLL + u)

        out_chunk(r, i).start()

    @pl.loop(0, NCHUNK)
    def _(i):
        out_chunk(r, i).wait()

    @pl.loop(0, COLS // 2)
    def _(q):
        for row in pair_rows(q):
            in_column(r, row, q).start()


def wait_columns(r, q):
    for row in pair_rows(q):
        in_column(r, row, q).wait()


def to_samples(columns, table):
    both = jnp.concatenate(thrice(columns(0), 0) + thrice(columns(1), 0), axis=0)
    return dot(table[...], both)


def record_pairs(r):
    flat, rec = r.flat, r.rec
    flat[0] = r.rec_in[:, :, 0:128]
    flat[1, :, :, 0 : NT - 128] = r.rec_in[:, :, 128:NT]
    flat[1, :, :, NT - 128 : 128] = jnp.zeros((SD, COLS, 256 - NT), F32)

    def row_copy(side, c):
        return pltpu.make_async_copy(
            flat.at[side, :, c, :], rec.at[side, c, pl.ds(0, SD)], r.rsem.at[side]
        )

    @pl.loop(0, COLS)
    def _(c):
        row_copy(0, c).start()
        row_copy(1, c).start()
        rec[0, c, SD:128, :] = jnp.zeros((128 - SD, 128), F32)
        rec[1, c, SD:128, :] = jnp.zeros((128 - SD, 128), F32)

    @pl.loop(0, COLS)
    def _(c):
        row_copy(0, c).wait()
        row_copy(1, c).wait()

    def pair_of(q):
        sides = [rec[side, pl.ds(2 * q, 2)].reshape(256, 128) for side in range(2)]
        return jnp.concatenate(sides, axis=1)

    return pair_of


def adjoint_spectrum(r):
    start_specs(r)
    spectra(r, 0, COLS // 2, record_pairs(r), r.forward_table, NT_DIMS)
    turn_rows(r, COLS // 2 - 1)
    wait_spectra(r)
    wait_specs(r)

    def step(w):
        ah, al = split(r.x[w][:, :SPAD])
        both = split(jnp.concatenate([r.sr[w], r.si[w]], axis=1))
        wide = dot(jnp.concatenate([ah, al], axis=0), both[0])
        p = wide[:ROWS2] + (wide[ROWS2:] + dot(ah, both[1]))
        r.y[w] = jnp.concatenate(
            [p[:COLS, :PD] + p[COLS:, PD:], p[COLS:, :PD] - p[:COLS, PD:]], axis=0
        )

    over_frequencies(r, step)


def adjoint_samples(r, first, last):
    @pl.loop(first, last)
    def _(q):
        wait_columns(r, q)
        res = to_samples(
            lambda part: jnp.concatenate(
                [r.xn[part * COLS + 2 * q], r.xn[part * COLS + 2 * q + 1]], axis=1
            ),
            r.inverse_table,
        )
        r.adj[2 * q] = res[:, :PD]
        r.adj[2 * q + 1] = res[:, PD:]


def weighted_table(r):
    table = r.forward_table
    high, low = split(dot3((table[:, 0:NT], table[:, 256 : 256 + NT]), split(r.prior[...])))
    r.weighted[...] = jnp.zeros_like(r.weighted)
    for i, piece in enumerate((high, low, high)):
        r.weighted[:, 256 * i : 256 * i + NT] = piece


def field_spectra(r, first, last):
    def pair_of(q):
        pair = jnp.concatenate([r.all_adj[2 * q], r.all_adj[2 * q + 1]], axis=1)
        return jnp.concatenate([pair, jnp.zeros((256 - NT, 256), F32)], axis=0)

    spectra(r, first, last, pair_of, r.weighted, ((1,), (0,)))
    turn_rows(r, last - 1)


def predicted_spectrum(r):
    wait_spectra(r)

    def step(w):
        f = r.x[w]
        re, im = f[:COLS], f[COLS:]
        fh, fl = split(f)
        left = jnp.concatenate(
            [jnp.concatenate([fh, fh], axis=1), jnp.concatenate([fl, jnp.zeros_like(fl)], axis=1)],
            axis=0,
        )
        prods = []
        for s in (r.sr, r.si):
            wide = dot(left, jnp.concatenate(split(s[w]), axis=1), NT_DIMS)
            prods.append(wide[:ROWS2] + wide[ROWS2:])
        p, q = prods
        r.y[w, :, 0:SPAD] = jnp.concatenate([p[:COLS] - q[COLS:], p[COLS:] + q[:COLS]], axis=0)

    over_frequencies(r, step)


def predicted_samples(r, g):
    for k in range(GROUP // 2):
        wait_columns(r, g * GROUP // 2 + k)
    res = to_samples(
        lambda part: jnp.concatenate(
            [r.xn[part * COLS + g * GROUP + k][:, :SPAD] for k in range(GROUP)], axis=1
        ),
        r.block_table,
    )
    r.p[g] = res.reshape(8, 2, SPADT, WIDE)


def selection(r):
    keys = r.pick.shape[1]
    where = r.place[...].reshape(1, keys)

    @pl.loop(0, 8)
    def _(i):
        at = pl.ds(pl.multiple_of(i * SPAD, SPAD), SPAD)
        row = lax.broadcasted_iota(jnp.int32, (SPAD, keys), 0)
        chosen = (row + i * SD == where) & (row < SD)
        r.pick[at, :] = chosen.astype(F32).astype(BF16)


def split_inverse(r):
    @pl.loop(0, STEPS)
    def _(t):
        high, low = split(r.inv[t])
        r.ih[t] = high
        r.il[t] = low


def put_in_order(r, g):
    left = jnp.concatenate(
        [
            jnp.concatenate([r.gath[g, i][:, k * SPAD : (k + 1) * SPAD] for i in range(8)], axis=1)
            for k in range(GROUP)
        ],
        axis=0,
    )
    high, low = split(left)
    res = dot(high, r.pick[...]) + dot(low, r.pick[...])
    for k in range(GROUP):
        r.perm[:, g * GROUP + k, :] = res[k * SPADT : (k + 1) * SPADT, :]


def apply_inverse(r):
    rows = r.ih.shape[1]
    r.u[...] = jnp.zeros_like(r.u)

    @pl.loop(0, STEPS)
    def _(t):
        r.u[:, 0:rows] += dot3(split(r.perm[t]), (r.ih[t], r.il[t]), NT_DIMS)


def sum_all(r, send, half, place, up, down, over):
    x, y_hi = place
    start = half * HALF_ROWS
    start_b = start + 8 * HALF_A
    size_b = 8 * QUARTER_B
    a, out = r.adj_rows, r.all_rows
    swap_a, swap_b, half_b, done_a = (
        ref.at[half] for ref in (r.swap_a, r.swap_b, r.half_b, r.done_a)
    )

    def at_a(q, h):
        return rows_at(start + (2 * q + h) * HALF_A, HALF_A)

    def at_half_b(q, h):
        return rows_at((2 * q + h) * QUARTER_B, QUARTER_B)

    def place_b(q, h):
        return rows_at(start_b + y_hi * size_b + (2 * q + h) * QUARTER_B, QUARTER_B)

    theirs = rows_at(start_b + (1 - y_hi) * size_b, size_b)
    ours = rows_at(start_b + y_hi * size_b, size_b)
    to_over_b = send(a.at[theirs], swap_b, over)
    ring_a = RingSum(send, a, at_a, x, up, down, r.relay_a.at[half], r.arrive_a.at[half])
    yield
    ring_a.pass_on()
    to_over_b.wait_recv()
    half_b[...] = a[ours] + swap_b[...]
    ring_b = RingSum(send, half_b, at_half_b, x, up, down, r.relay_b.at[half], r.arrive_b.at[half])
    yield
    for h in range(2):
        done_a[h] = ring_a.half(h)
    to_over_a = send(done_a.at[1 - y_hi], swap_a, over)
    ring_b.pass_on()
    yield
    to_over_a.wait_recv()
    mine = at_a(x, y_hi)
    out[mine] = done_a[y_hi] + swap_a[...]
    back_a = send(out.at[mine], out.at[mine], over)
    for h in range(2):
        out[place_b(x, h)] = ring_b.half(h)
    spread_b = RingSpread(send, out, place_b, x, up, down)
    yield
    back_a.wait_recv()
    spread_a = RingSpread(send, out, at_a, x, up, down)
    spread_b.pass_on()
    yield
    spread_b.finish()
    back_b = send(out.at[ours], out.at[ours], over)
    spread_a.pass_on()
    yield
    spread_a.finish()
    back_b.wait_recv()
    yield


def sum_times(r, send, g, place, links):
    x, y_hi, y_lo, z, core = place
    next_z, last_z, beside, partner = links[:4]
    p, core_in, mine, own, swap, out = (
        ref.at[g] for ref in (r.p, r.core_in, r.mine, r.own, r.swap_t, r.gath)
    )
    order = [(h, (z + d) % 4) for d, h in ((2, 0), (2, 1), (1, 1), (3, 0), (1, 0), (3, 1), (0, 0), (0, 1))]
    swaps = [send(p.at[4 * h + q, 1 - core], core_in.at[4 * h + q], partner) for h, q in order]
    yield
    for copy, (h, q) in zip(swaps, order):
        m = 4 * h + q
        copy.wait_recv()
        mine[m] = p[m, core] + core_in[m]
    ring = RingSum(
        send, mine, lambda q, h: 4 * h + q, z, next_z, last_z, r.relay_t.at[g], r.arrive_t.at[g]
    )
    yield
    ring.pass_on()
    yield
    for h in range(2):
        own[h] = ring.half(h)
    to_beside = send(own.at[1 - y_lo], swap, beside)
    yield
    to_beside.wait_recv()
    sens = 2 * x + y_hi
    out[sens] = own[y_lo] + swap[...]

    copies = [send(out.at[sens], out.at[sens], to) for to in links[4:]]
    yield
    for copy in copies:
        copy.wait_recv()
    yield


def finish(r, send, others, sens, me):
    for c in range(COLS):
        r.rows[c] = jnp.broadcast_to(r.u[c : c + 1, :], (8, 128))
    sent = [send(r.rows.at[j], r.recv.at[d], (sens, j)) for d, j in enumerate(others)]
    total = r.rows[me]
    for d, copy in enumerate(sent):
        copy.wait_recv()
        total = total + r.recv[d]
    r.out[...] = total[0:1, 0 : r.out.shape[1]]


INPUTS = [
    "rec_in",
    "sr_hbm",
    "si_hbm",
    "prior",
    "place",
    "inv_hbm",
    "forward_table",
    "inverse_table",
    "block_table",
]
OUTPUTS = ["out", "rows_hbm", "freq_hbm"]


def scratch(keys, rows):
    dma = pltpu.SemaphoreType.DMA
    part = (HALVES,)
    t_block = (SPADT, WIDE)
    messages = 150
    return dict(
        sr=pltpu.VMEM((NF, SPAD, PD), F32),
        si=pltpu.VMEM((NF, SPAD, PD), F32),
        x=pltpu.VMEM((NF, ROWS2, 128), F32),
        y=pltpu.VMEM((NF, ROWS2, 128), F32),
        xn=pltpu.VMEM((ROWS2, 256, 128), F32),
        flat=pltpu.VMEM((2, SD, COLS, 128), F32),
        rec=pltpu.VMEM((2, COLS, 128, 128), F32),
        adj=pltpu.VMEM((COLS, NT, PD), F32),
        all_adj=pltpu.VMEM((COLS, NT, PD), F32),
        weighted=pltpu.VMEM((2 * FR, 768), BF16),
        relay_a=pltpu.VMEM((*part, 2, HALF_A, 128), F32),
        arrive_a=pltpu.VMEM((*part, 4, HALF_A, 128), F32),
        swap_a=pltpu.VMEM((*part, HALF_A, 128), F32),
        done_a=pltpu.VMEM((*part, 2, HALF_A, 128), F32),
        relay_b=pltpu.VMEM((*part, 2, QUARTER_B, 128), F32),
        arrive_b=pltpu.VMEM((*part, 4, QUARTER_B, 128), F32),
        swap_b=pltpu.VMEM((*part, 8 * QUARTER_B, 128), F32),
        half_b=pltpu.VMEM((*part, 8 * QUARTER_B, 128), F32),
        p=pltpu.VMEM((*part, 8, 2, *t_block), F32),
        core_in=pltpu.VMEM((*part, 8, *t_block), F32),
        mine=pltpu.VMEM((*part, 8, *t_block), F32),
        relay_t=pltpu.VMEM((*part, 2, *t_block), F32),
        arrive_t=pltpu.VMEM((*part, 4, *t_block), F32),
        own=pltpu.VMEM((*part, 2, *t_block), F32),
        swap_t=pltpu.VMEM((*part, *t_block), F32),
        gath=pltpu.VMEM((*part, 8, *t_block), F32),
        pick=pltpu.VMEM((8 * SPAD, keys), BF16),
        inv=pltpu.VMEM((STEPS, rows, keys), F32),
        ih=pltpu.VMEM((STEPS, rows, keys), BF16),
        il=pltpu.VMEM((STEPS, rows, keys), BF16),
        perm=pltpu.VMEM((SPADT, COLS, keys), F32),
        u=pltpu.VMEM((COLS, 128), F32),
        rows=pltpu.VMEM((COLS, 8, 128), F32),
        recv=pltpu.VMEM((COLS - 1, 8, 128), F32),
        spec_sem=dma((2,)),
        rsem=dma((2,)),
        xsem=dma((2, COLS // 2)),
        ysem=dma((NCHUNK,)),
        csem=dma((COLS // 2,)),
        inv_sem=dma,
        ssem=dma((messages,)),
        msem=dma((messages,)),
    )


def kernel(names, *refs):
    r = Refs(names, refs)
    r.adj_rows = r.adj.reshape(COLS * NT, PD)
    r.all_rows = r.all_adj.reshape(COLS * NT, PD)
    x, y_hi, y_lo, z, core = place = here()
    sens, me = lax.axis_index("sens"), lax.axis_index("par")
    up = device((x + 1) % 4, y_hi, y_lo, z, core)
    down = device((x + 3) % 4, y_hi, y_lo, z, core)
    over = device(x, 1 - y_hi, y_lo, z, core)
    next_z = device(x, y_hi, y_lo, (z + 1) % 4, core)
    last_z = device(x, y_hi, y_lo, (z + 3) % 4, core)
    beside = device(x, y_hi, 1 - y_lo, z, core)
    partner = device(x, y_hi, y_lo, z, 1 - core)
    others = [(me + d) % COLS for d in range(1, COLS)]
    friends = [(sens, j) for j in others]
    around = [device((x + d) % 4, (y_hi + e) % 2, y_lo, z, core) for e, d in PEERS]
    friends += around
    links = (next_z, last_z, beside, partner, *around)
    greet(friends)
    send = Sender(r.ssem, r.msem)
    adjoint_spectrum(r)
    inverse = pltpu.make_async_copy(r.inv_hbm, r.inv, r.inv_sem)
    inverse.start()
    weighted_table(r)
    pairs = COLS // 2 // HALVES
    adjoint_samples(r, 0, pairs)
    all_here(friends)
    first = sum_all(r, send, 0, (x, y_hi), up, down, over)
    next(first)
    adjoint_samples(r, pairs, 2 * pairs)
    second = sum_all(r, send, 1, (x, y_hi), up, down, over)
    next(second)
    for _ in range(4):
        next(first)
        next(second)
    next(first)
    next(second)
    next(first)
    field_spectra(r, 0, pairs)
    next(second)
    field_spectra(r, pairs, 2 * pairs)
    inverse.wait()
    split_inverse(r)
    selection(r)
    predicted_spectrum(r)
    predicted_samples(r, 0)
    first = sum_times(r, send, 0, place, links)
    next(first)
    predicted_samples(r, 1)
    second = sum_times(r, send, 1, place, links)
    next(second)
    for step in range(3):
        next(first)
        next(second)
    for step in range(1):
        next(first)
        next(second)
    next(first)
    put_in_order(r, 0)
    next(second)
    put_in_order(r, 1)
    apply_inverse(r)
    finish(r, send, others, sens, me)
    send.finish()


def shards(records, spec_real, spec_imag, prior_cov, sensor_map, inverse_rows):
    tabs = tables()
    sr, si = spec_real.transpose(1, 0, 2), spec_imag.transpose(1, 0, 2)
    rows, _, keys = inverse_rows.shape
    spaces = scratch(keys, rows)
    out, _, _ = pl.pallas_call(
        functools.partial(kernel, INPUTS + OUTPUTS + list(spaces)),
        out_shape=(
            jax.ShapeDtypeStruct((1, rows), F32),
            jax.ShapeDtypeStruct((ROWS2, NF, 128), F32),
            jax.ShapeDtypeStruct((NF, ROWS2, 128), F32),
        ),
        in_specs=[VMEM, ANY, ANY, VMEM, VMEM, ANY] + [VMEM] * 3,
        out_specs=(VMEM, HBM, HBM),
        scratch_shapes=list(spaces.values()),
        compiler_params=pltpu.CompilerParams(
            vmem_limit_bytes=LIMIT, collective_id=0, has_side_effects=True
        ),
        name="tsunami",
    )(records.transpose(1, 0, 2), sr, si, prior_cov, sensor_map, inverse_rows.transpose(1, 0, 2), *tabs)
    return out


def solution(mesh):
    return jax.shard_map(
        shards,
        mesh=mesh,
        in_specs=(
            P(None, "sens", None),
            P(None, "sens", "par"),
            P(None, "sens", "par"),
            P(),
            P(),
            P("sens", "par", None),
        ),
        out_specs=P("par", "sens"),
        check_vma=False,
    )
```
